32 devices in a mesh: ep: 4 (over z), rep: 4 (over y, core), opt: 2 (over x).
Axes of the slice: x: 2, y: 2, z: 4, core: 2. Of those that a mesh axis runs over, the one named last changes fastest.
Arguments:
- incoming_tokens: bfloat16 [4, 4, 2, 128, 2048], P('ep', 'rep', None, None, 'opt'), may hold values from -6 to 6
- cotangent: bfloat16 [4, 4, 2, 128, 2048], P('ep', 'rep', None, None, 'opt'), may hold values from -6 to 6
- block_dest: int32 [4, 4, 2], replicated, may hold values from 0 to 3, as said below
- gate_weight: bfloat16 [4, 2048, 768], P('ep'), may hold values from -0.125 to 0.125
- up_weight: bfloat16 [4, 2048, 768], P('ep'), may hold values from -0.125 to 0.125
- basis: bfloat16 [4, 768, 512], P('ep'), may hold values from -0.21875 to 0.21875
- moment_first: float32 [4, 512, 2048], P('ep', 'rep', 'opt'), may hold values from -6 to 6
- moment_second: float32 [4, 512, 2048], P('ep', 'rep', 'opt'), may hold values from 0.05 to 1
Outputs:
- first_moment: float32 [4, 512, 2048], P('ep', 'rep', 'opt')
- second_moment: float32 [4, 512, 2048], P('ep', 'rep', 'opt')
- weight_delta: bfloat16 [4, 768, 2048], P('ep', None, 'opt')
The draws below stay inside these ranges and needn't reach their ends.
Inputs may be any that keep to these rules, and one draw needn't show every extreme that they name: `block_dest`: the 2 blocks of one pair of indices (s, r) go to 2 different instances.
All inputs are finite; a program needn't handle non-finite values.
Results may differ from the reference program's by a relative error of at most 0.0085.
Values may be sent and summed in bfloat16 or wider, within the bound.
No kernel may reach another device: no remote copies, remote signals or barrier semaphores. Data moves between devices by JAX's collectives and lax.ppermute only.
A program may use at most 64 MiB of HBM per device.

```python
import math
import jax
import jax.numpy as jnp
from jax import lax

D = 2048
FF = 768
RANK = 512
BLOCK_ROWS = 128
INSTANCES = 4
REPLICAS = 4
BLOCKS = 2
N_EP = 4
N_REP = 4


def draw_block_dest(key, part):
    heat_key, score_key = jax.random.split(jax.random.fold_in(key, 17))
    instance_heat = jax.random.randint(heat_key, (N_EP,), 0, 4) * 512
    scores = jax.random.randint(score_key, (N_EP, N_REP, N_EP), 0, 1024) + instance_heat[None, None, :]
    distinct = scores * N_EP + jnp.arange(N_EP, dtype=jnp.int32)[None, None, :]
    return lax.top_k(distinct, BLOCKS)[1].astype(jnp.int32)


def block_scale(stream_key, extent, pieces, least, high):
    loudness = 1.0
    for axis_at, shards_of in pieces:
        draws = jax.random.uniform(jax.random.fold_in(jax.random.fold_in(stream_key, 6), axis_at), (shards_of,), jnp.float32, least / len(pieces), high / len(pieces))
        loudness = loudness * jnp.repeat(jnp.exp(draws), extent[axis_at] // shards_of).reshape((-1,) + (1,) * (len(extent) - 1 - axis_at))
    return loudness


def normal_values(own_key, extent, width, reach, shards=(), held_as=jnp.bfloat16):
    result = width * jax.random.normal(own_key, extent, jnp.float32)
    if shards:
        result = result * block_scale(own_key, extent, shards, -0.22, 0.18)
    return jnp.clip(result, -reach, reach).astype(held_as)


def setup_inputs(seed: int = 0) -> dict:
    seeds = jax.random.split(jax.random.key(seed), 9)
    incoming_tokens = normal_values(seeds[0], (INSTANCES, REPLICAS, BLOCKS, BLOCK_ROWS, D), 1.0, 6.0, ((0, 4), (1, 4), (4, 2)))
    cotangent = normal_values(seeds[1], (INSTANCES, REPLICAS, BLOCKS, BLOCK_ROWS, D), 1.0, 6.0, ((0, 4), (1, 4), (4, 2)))
    block_dest = draw_block_dest(jax.random.fold_in(seeds[8], 71), 0)
    gate_weight = normal_values(seeds[3], (INSTANCES, D, FF), D ** -0.5, 0.125, ((0, 4),))
    up_weight = normal_values(seeds[4], (INSTANCES, D, FF), D ** -0.5, 0.125, ((0, 4),))
    basis = normal_values(seeds[5], (INSTANCES, FF, RANK), FF ** -0.5, 0.21875, ((0, 4),))
    moment_first = normal_values(seeds[6], (INSTANCES, RANK, D), 1.0, 6.0, ((0, 4), (1, 4), (2, 2)), jnp.float32)
    moment_second = jnp.clip(jnp.exp(math.log(1.0) - 2.9957323 * jax.random.uniform(seeds[7], (INSTANCES, RANK, D), jnp.float32) ** block_scale(seeds[7], (INSTANCES, RANK, D), ((0, 4), (1, 4), (2, 2)), -0.2, 0.2)), 0.05, 1.0)
    return dict(incoming_tokens=incoming_tokens, cotangent=cotangent, block_dest=block_dest, gate_weight=gate_weight, up_weight=up_weight, basis=basis, moment_first=moment_first, moment_second=moment_second)


beta_one = 0.9
beta_two = 0.999
adam_step = 1000.0
adam_eps = 1e-08

def reference(incoming_tokens, cotangent, block_dest, gate_weight, up_weight, basis, moment_first, moment_second):
    flat_tokens = incoming_tokens.reshape(-1, BLOCK_ROWS, D)
    flat_cotangent = cotangent.reshape(-1, BLOCK_ROWS, D)
    flat_dest = block_dest.reshape(-1).astype(jnp.int32)

    def accumulate(running_total, item):
        block_tokens, block_cotangent, target_value = item
        gate_values = jnp.dot(block_tokens, gate_weight[target_value], preferred_element_type=jnp.float32)
        up_values = jnp.dot(block_tokens, up_weight[target_value], preferred_element_type=jnp.float32)
        hidden = (jax.nn.silu(gate_values) * up_values).astype(jnp.bfloat16)
        projected = jnp.dot(hidden, basis[target_value], preferred_element_type=jnp.float32).astype(jnp.bfloat16)
        contribution = jnp.dot(projected.T, block_cotangent, preferred_element_type=jnp.float32)
        current = lax.dynamic_index_in_dim(running_total, target_value, 0, keepdims=False)
        running_total = lax.dynamic_update_index_in_dim(running_total, current + contribution, target_value, 0)
        return (running_total, None)
    gradients, _ = lax.scan(accumulate, jnp.zeros((N_EP, RANK, D), jnp.float32), (flat_tokens, flat_cotangent, flat_dest))
    first_moment = beta_one * moment_first + (1.0 - beta_one) * gradients
    second_moment = beta_two * moment_second + (1.0 - beta_two) * gradients * gradients
    scaled_first = first_moment / (1.0 - beta_one ** adam_step)
    scaled_second = second_moment / (1.0 - beta_two ** adam_step)
    update = (-scaled_first / (jnp.sqrt(scaled_second) + adam_eps)).astype(jnp.bfloat16)
    weight_change = jnp.einsum('efr,erd->efd', basis.astype(jnp.float32), update.astype(jnp.float32), precision=lax.Precision.HIGHEST)
    return (first_moment, second_moment, weight_change.astype(jnp.bfloat16))
```

```python
import jax
import jax.numpy as jnp
from jax import lax
from jax.sharding import PartitionSpec as P

beta_one = 0.9
beta_two = 0.999
adam_step = 1000.0
adam_eps = 1e-08


SWAP_MOST = 4
SHARES = (2, 1, 1)
LANES = 128


def swap(value, axis, distance):
    count = lax.axis_size(axis)
    return lax.ppermute(value, axis, [(i, i ^ distance) for i in range(count)])


def by_pairs(count):
    return count <= SWAP_MOST and count & (count - 1) == 0


def far_first(count):
    return list(range(2, count)) + [1] if count > 2 else list(range(1, count))


def exchange(pieces, axis):
    count = len(pieces)
    if by_pairs(count):
        got = {k: swap(pieces[k], axis, k) for k in far_first(count)}
        return [pieces[0]] + [got[k] for k in range(1, count)]
    got = lax.all_to_all(jnp.stack(pieces), axis, split_axis=0, concat_axis=0, tiled=True)
    return [got[k] for k in range(count)]


def peer_of(axis, k):
    return lax.axis_index(axis) ^ k if by_pairs(lax.axis_size(axis)) else jnp.int32(k)


def bit_order(count):
    order = [0]
    while len(order) < count:
        order = [2 * j for j in order] + [2 * j + 1 for j in order]
    return order


def column_chunks(width):
    unit = width // sum(SHARES)
    if unit % LANES:
        return [(0, width)]
    stops = [sum(SHARES[: i + 1]) * unit for i in range(len(SHARES))]
    return list(zip([0] + stops[:-1], stops))


def shards(
    incoming_tokens,
    cotangent,
    block_dest,
    gate_weight,
    up_weight,
    basis,
    moment_first,
    moment_second,
):
    ep_index = lax.axis_index("ep")
    rep_index = lax.axis_index("rep")
    opt_index = lax.axis_index("opt")
    ep_count = lax.axis_size("ep")
    rep_count = lax.axis_size("rep")
    opt_count = lax.axis_size("opt")
    tokens = incoming_tokens[0, 0]
    cot = cotangent[0, 0]
    blocks, rows, width = tokens.shape
    part = rows // opt_count
    rank_block = moment_first.shape[1]
    chunks = column_chunks(width)

    rep_plane = lax.dynamic_index_in_dim(block_dest, rep_index, 1, keepdims=False)
    own_dest = lax.dynamic_index_in_dim(rep_plane, ep_index, 0, keepdims=False)
    senders = [peer_of("ep", k) for k in range(ep_count)]

    def for_peers(values):
        result = []
        for k in range(ep_count):
            block = values[0]
            for b in range(1, blocks):
                block = jnp.where(own_dest[b] == senders[k], values[b], block)
            result.append(block)
        return result

    row_part = [
        lax.dynamic_slice_in_dim(tokens, peer_of("opt", j) * part, part, axis=1)
        for j in range(opt_count)
    ]
    features = exchange(row_part, "opt")
    gate_values = 0.0
    up_values = 0.0
    groups = [[j] for j in range(opt_count)] if by_pairs(opt_count) else [list(range(opt_count))]
    for group in groups:
        mine = features[group[0]] if len(group) == 1 else jnp.concatenate([features[j] for j in group], axis=2)
        slots = jnp.concatenate(exchange(for_peers(mine), "ep"), axis=0)
        size = width * len(group)
        at = peer_of("opt", group[0]) * width
        gate_part = lax.dynamic_slice_in_dim(gate_weight[0], at, size, axis=0)
        up_part = lax.dynamic_slice_in_dim(up_weight[0], at, size, axis=0)
        gate_values += jnp.dot(slots, gate_part, preferred_element_type=jnp.float32)
        up_values += jnp.dot(slots, up_part, preferred_element_type=jnp.float32)
    flags = jnp.stack(
        [
            jnp.any(lax.dynamic_index_in_dim(rep_plane, sender, 0, keepdims=False) == ep_index)
            for sender in senders
        ]
    )
    hidden = (jax.nn.silu(gate_values) * up_values).astype(jnp.bfloat16)
    order = bit_order(rep_count)
    basis_blocks = jnp.concatenate(
        [lax.dynamic_slice_in_dim(basis[0], (rep_index ^ j) * rank_block, rank_block, axis=1) for j in order],
        axis=1,
    )
    projected = jnp.dot(hidden, basis_blocks, preferred_element_type=jnp.float32)
    rank = projected.shape[1]
    projected = projected.reshape(ep_count, part, rank)
    projected = jnp.where(flags[:, None, None], projected, 0.0).astype(jnp.bfloat16)
    if by_pairs(opt_count):
        pieces = [projected] + [swap(projected, "opt", j) for j in range(1, opt_count)]
        pieces = [select_piece(pieces, opt_index, q) for q in range(opt_count)]
        projected_rows = jnp.stack(pieces, axis=1).reshape(ep_count * rows, rank)
    else:
        projected_rows = lax.all_gather(projected, "opt", axis=1, tiled=True).reshape(-1, rank)

    gradients = []
    updates = []
    for at, (start, stop) in enumerate(chunks):
        cot_rows = jnp.concatenate(exchange(for_peers(cot[:, :, start:stop]), "ep"), axis=0)
        kept = rank
        current = None
        bit = 1
        while bit < rep_count:
            kept //= 2
            if current is None:
                current = lax.dot_general(
                    projected_rows[:, :kept], cot_rows, (((0,), (0,)), ((), ())), preferred_element_type=jnp.float32
                )
                outgoing = lax.dot_general(
                    projected_rows[:, kept:], cot_rows, (((0,), (0,)), ((), ())), preferred_element_type=jnp.float32
                )
            else:
                outgoing = current[kept:]
                current = current[:kept]
            current = current + swap(outgoing.astype(jnp.bfloat16), "rep", bit).astype(jnp.float32)
            bit *= 2
        gradient = current
        gradients.append(gradient)
        first = beta_one * moment_first[0, :, start:stop] + (1.0 - beta_one) * gradient
        second = beta_two * moment_second[0, :, start:stop] + (1.0 - beta_two) * gradient * gradient
        scaled_first = first / (1.0 - beta_one**adam_step)
        scaled_second = second / (1.0 - beta_two**adam_step)
        update = (-scaled_first / (jnp.sqrt(scaled_second) + adam_eps)).astype(jnp.bfloat16)
        bit = rep_count // 2
        while bit:
            update = jnp.concatenate([update, swap(update, "rep", bit)], axis=0)
            bit //= 2
        updates.append(update)
    gradient = jnp.concatenate(gradients, axis=1)
    first_moment = beta_one * moment_first[0] + (1.0 - beta_one) * gradient
    second_moment = beta_two * moment_second[0] + (1.0 - beta_two) * gradient * gradient
    weight_change = jnp.dot(basis_blocks, jnp.concatenate(updates, axis=1), preferred_element_type=jnp.float32)
    return (first_moment[None], second_moment[None], weight_change.astype(jnp.bfloat16)[None])


def select_piece(pieces, index, target):
    result = pieces[0]
    for j in range(1, len(pieces)):
        result = jnp.where((index ^ target) == j, pieces[j], result)
    return result


def solution(mesh):
    in_specs = (
        P("ep", "rep", None, None, "opt"),
        P("ep", "rep", None, None, "opt"),
        P(),
        P("ep", None, None),
        P("ep", None, None),
        P("ep", None, None),
        P("ep", "rep", "opt"),
        P("ep", "rep", "opt"),
    )
    out_specs = (P("ep", "rep", "opt"), P("ep", "rep", "opt"), P("ep", None, "opt"))

    return jax.shard_map(shards, mesh=mesh, in_specs=in_specs, out_specs=out_specs, check_vma=False)
```
